256 devices in a mesh: dp: 8 (over z), ctx: 32 (over y, x, core).
Axes of the slice: x: 4, y: 4, z: 8, core: 2. Of those that a mesh axis runs over, the one named last changes fastest.
Arguments:
- queries: bfloat16 [8, 4096, 2048], P('dp', 'ctx'), may hold values from -6 to 6
- keys: bfloat16 [8, 4096, 2048], P('dp', 'ctx'), may hold values from -6 to 6
- values: bfloat16 [8, 4096, 2048], P('dp', 'ctx'), may hold values from -6 to 6
- grad_output: bfloat16 [8, 4096, 2048], P('dp', 'ctx'), may hold values from -6 to 6
- out_gain: float32 [2048], replicated, may hold values from 0.5 to 1.5
- doc_lengths: int32 [8, 12], P('dp'), may hold values from 1 to 1365, 4096 in all within a row
Outputs:
- output: bfloat16 [8, 4096, 2048], P('dp', 'ctx')
- grad_queries: bfloat16 [8, 4096, 2048], P('dp', 'ctx')
- grad_keys: bfloat16 [8, 4096, 2048], P('dp', 'ctx')
- grad_values: bfloat16 [8, 4096, 2048], P('dp', 'ctx')
- grad_gain: float32 [2048], replicated
The draws below stay inside these ranges and needn't reach their ends.
Inputs may be any that keep to these rules, and one draw needn't show every extreme that they name: `doc_lengths`: each row holds the lengths of 12 documents packed end to end; they sum to 4096, and the largest is exactly 1365.
All inputs are finite; a program needn't handle non-finite values.
Results may differ from the reference program's by a relative error of at most 0.012.
The reference program's roundings to bfloat16 on the way count: a program that leaves them out, or rounds other values in their place, can miss the bound.
Values may be sent and summed in bfloat16 or wider, within the bound.
No kernel may reach another device: no remote copies, remote signals or barrier semaphores. Data moves between devices by JAX's collectives and lax.ppermute only.
A program may use at most 64 MiB of HBM per device.

```python
import math
import jax
import jax.numpy as jnp
import numpy as np
from jax import lax

H = 32
E = 64
DOCS = 12
BATCH = 8
LEN = 4096
BLK = 128
HE = 2048


def shard_levels(rng, extent, cuts, low, largest):
    factor_of, own = 1.0, jax.random.fold_in(rng, 6)
    for dim, blocks in cuts:
        heights = jnp.exp(jax.random.uniform(jax.random.fold_in(own, dim), (blocks,), jnp.float32, low / len(cuts), largest / len(cuts)))
        factor_of = factor_of * jnp.repeat(heights, extent[dim] // blocks).reshape([-1 if axis == dim else 1 for axis in range(len(extent))])
    return factor_of


def profile(number_of, total, reach, slope):
    loads = [(1 << 20) // math.isqrt(rank ** slope) + 1 for rank in range(2, number_of + 1)]
    surplus, given = total - reach - (number_of - 1), [1] * (number_of - 1)
    while surplus > 0:
        candidates = [i for i in range(number_of - 1) if given[i] < reach]
        whole, budget = sum([loads[i] for i in candidates]), surplus
        for i in candidates:
            extra = min(reach - given[i], max(1, budget * loads[i] // whole), surplus)
            given[i] = given[i] + extra
            surplus = surplus - extra
    return np.array([reach] + given)


def ragged(rng, count, total, most, lean):
    if count == 2:
        one = jax.random.randint(rng, (), max(1, total - most), min(most, total - 1) + 1)
        return jnp.stack([one, total - one])
    tallies = jnp.asarray(profile(count, total, most, lean), jnp.int32)
    pairs = (count - 1) // 2
    donor, sink = tallies[1:1 + 2 * pairs:2], tallies[2:2 + 2 * pairs:2]
    margin = jnp.minimum(donor - 1, most - sink)
    shifted = jax.random.randint(jax.random.fold_in(rng, 1), (pairs,), 0, 1 << 20) % (margin + 1)
    tallies = tallies.at[1:1 + 2 * pairs:2].set(donor - shifted).at[2:2 + 2 * pairs:2].set(sink + shifted)
    return tallies[jax.random.permutation(jax.random.fold_in(rng, 2), count)]


def bell_draw(rng, shape, width, bound, cuts=(), kind=jnp.bfloat16):
    level = shard_levels(rng, shape, cuts, -0.22, 0.18) if cuts else 1.0
    result = jax.random.normal(rng, shape, jnp.float32) * width * level
    return jnp.minimum(jnp.maximum(result, -bound), bound).astype(kind)


def setup_inputs(seed: int = 0) -> dict:
    splits = jax.random.split(jax.random.key(seed), 7)
    return {
        "queries": bell_draw(splits[0], (BATCH, LEN, HE), 1.0, 6.0, ((0, 8), (1, 32))),
        "keys": bell_draw(splits[1], (BATCH, LEN, HE), 1.0, 6.0, ((0, 8), (1, 32))),
        "values": bell_draw(splits[2], (BATCH, LEN, HE), 1.0, 6.0, ((0, 8), (1, 32))),
        "grad_output": bell_draw(splits[3], (BATCH, LEN, HE), 1.0, 6.0, ((0, 8), (1, 32))),
        "out_gain": jnp.clip(1.0 + 0.1 * jax.random.normal(splits[4], (HE,), jnp.float32), 0.5, 1.5),
        "doc_lengths": jax.vmap(lambda own: ragged(own, DOCS, LEN, LEN // 3, 2))(jax.random.split(splits[5], BATCH)).reshape((BATCH, DOCS)).astype(jnp.int32),
    }


eps = 1e-05
precise = lax.Precision.HIGHEST

def geometry(length_row):
    doc_ends = jnp.cumsum(length_row).astype(jnp.int32)
    begins = (doc_ends - length_row).astype(jnp.int32)
    positions = jnp.arange(LEN, dtype=jnp.int32)
    doc_ids = lax.optimization_barrier(jnp.sum((positions[:, None] >= doc_ends[None, :]).astype(jnp.int32), axis=1)).astype(jnp.int32)
    starts = lax.optimization_barrier(jnp.sum((positions[:, None] == begins[None, :]).astype(jnp.float32), axis=1))
    return (doc_ids, starts)

def chain_step(carried, pieces):
    state_piece, open_piece = pieces
    return (state_piece + (1.0 - open_piece) * carried, carried)

def reference(queries, keys, values, grad_output, out_gain, doc_lengths):
    nblocks = LEN // BLK
    gain_heads = out_gain.reshape(H, E)

    def one_sequence(packed):
        qs, ks, vs, gs, length_row = packed
        doc_ids, starts = geometry(length_row)
        doc_ids = doc_ids.reshape(nblocks, BLK)
        starts = starts.reshape(nblocks, BLK)
        shape4 = (nblocks, BLK, H, E)
        qf = qs.reshape(shape4).astype(jnp.float32)
        kf = ks.reshape(shape4).astype(jnp.float32)
        vf = vs.reshape(shape4).astype(jnp.float32)
        dyf = gs.reshape(shape4).astype(jnp.float32)
        counted = jnp.cumsum(starts, axis=1)
        totals = counted[:, -1:]
        before = (counted == 0).astype(jnp.float32)[:, :, None, None]
        after_mask = (totals - counted == 0).astype(jnp.float32)[:, :, None, None]
        opened = jnp.minimum(totals[:, 0], 1.0)
        row_ids = jnp.arange(BLK)
        causal = row_ids[:, None] >= row_ids[None, :]
        doc_mask = jnp.logical_and(causal[None], doc_ids[:, :, None] == doc_ids[:, None, :]).astype(jnp.float32)[:, None]
        scores = jnp.einsum('btge,bsge->bgts', qf, kf, precision=precise) * doc_mask
        weights = lax.optimization_barrier(scores.astype(jnp.bfloat16)).astype(jnp.float32)
        own_state = jnp.einsum('bsge,bsgf->bgef', kf * after_mask, vf, precision=precise)
        zero_state = jnp.zeros((H, E, E), jnp.float32)
        _, carried = lax.scan(chain_step, zero_state, (own_state, opened))
        attended = jnp.einsum('bgts,bsgf->btgf', weights, vf, precision=precise)
        attended = attended + before * jnp.einsum('btge,bgef->btgf', qf, carried, precision=precise)
        root_mean = jnp.sqrt(lax.optimization_barrier(jnp.mean(attended * attended, axis=-1, keepdims=True)) + eps)
        normed = attended / root_mean
        output = (gain_heads * normed).astype(jnp.bfloat16)
        dnormed = dyf * gain_heads
        grad_att = (dnormed - normed * lax.optimization_barrier(jnp.mean(dnormed * normed, axis=-1, keepdims=True))) / root_mean
        grad_att = lax.optimization_barrier(grad_att.astype(jnp.bfloat16)).astype(jnp.float32)
        gain_part = lax.optimization_barrier(jnp.sum(dyf * normed, axis=(0, 1)))
        grad_scores = jnp.einsum('btgf,bsgf->bgts', grad_att, vf, precision=precise) * doc_mask
        grad_weights = lax.optimization_barrier(grad_scores.astype(jnp.bfloat16)).astype(jnp.float32)
        back_state = jnp.einsum('btge,btgf->bgef', qf * before, grad_att, precision=precise)
        _, back_carried = lax.scan(chain_step, zero_state, (back_state, opened), reverse=True)
        grad_q = jnp.einsum('bgts,bsge->btge', grad_weights, kf, precision=precise)
        grad_q = grad_q + before * jnp.einsum('btgf,bgef->btge', grad_att, carried, precision=precise)
        grad_k = jnp.einsum('bgts,btge->bsge', grad_weights, qf, precision=precise)
        grad_k = grad_k + after_mask * jnp.einsum('bsgf,bgef->bsge', vf, back_carried, precision=precise)
        grad_v = jnp.einsum('bgts,btgf->bsgf', weights, grad_att, precision=precise)
        grad_v = grad_v + after_mask * jnp.einsum('bsge,bgef->bsgf', kf, back_carried, precision=precise)
        flat = (LEN, H * E)
        return (output.reshape(flat), grad_q.astype(jnp.bfloat16).reshape(flat), grad_k.astype(jnp.bfloat16).reshape(flat), grad_v.astype(jnp.bfloat16).reshape(flat), gain_part)
    outs = lax.map(one_sequence, (queries, keys, values, grad_output, doc_lengths))
    grad_gain = lax.optimization_barrier(jnp.sum(outs[4], axis=0)).reshape(H * E) / math.sqrt(BATCH * LEN)
    return (outs[0], outs[1], outs[2], outs[3], grad_gain)
```

```python
import math

import jax
import jax.numpy as jnp
from jax import lax
from jax.experimental import pallas as pl
from jax.experimental.pallas import tpu as pltpu
from jax.sharding import PartitionSpec as P

H = 32
E = 64
PAIR = 2 * E
PAIRS = H // 2
DOCS = 12
BLK = 128
NBLK = 32
ROWS = 32
WIDE = 48

eps = 1e-05
f32 = jnp.float32
bf16 = jnp.bfloat16


def dot(a, b):
    return lax.dot_general(a, b, (((1,), (0,)), ((), ())), preferred_element_type=f32)


def dot_nt(a, b):
    return lax.dot_general(a, b, (((1,), (1,)), ((), ())), preferred_element_type=f32)


def dot_tn(a, b):
    return lax.dot_general(a, b, (((0,), (0,)), ((), ())), preferred_element_type=f32)


def bounds(len_ref):
    begins, total = [], jnp.int32(0)
    for k in range(DOCS):
        begins.append(total)
        total = total + len_ref[0, k]
    return begins


def block_masks(begins, base):
    shape = (BLK, BLK)
    row = lax.broadcasted_iota(jnp.int32, shape, 0) + base
    col = lax.broadcasted_iota(jnp.int32, shape, 1) + base
    row_id = jnp.zeros(shape, jnp.int32)
    col_id = jnp.zeros(shape, jnp.int32)
    first_id = jnp.int32(0)
    last_id = jnp.int32(0)
    for begin in begins:
        row_id = row_id + (row >= begin).astype(jnp.int32)
        col_id = col_id + (col >= begin).astype(jnp.int32)
        first_id = first_id + (begin < base).astype(jnp.int32)
        last_id = last_id + (begin < base + BLK).astype(jnp.int32)
    doc_mask = jnp.logical_and(row >= col, row_id == col_id)
    before = row_id == first_id
    after = row_id == last_id
    return doc_mask, before, after


def halves():
    return lax.broadcasted_iota(jnp.int32, (BLK, PAIR), 1) < E


def pick(cond, a):
    return jnp.where(cond, a, jnp.zeros_like(a))


def heads(left, a):
    return jnp.concatenate([pick(left, a), pick(jnp.logical_not(left), a)], axis=0)


def squeeze_state(left, full):
    return jnp.where(left[:E], full[:E], full[E:])


def spread_state(left, state):
    return jnp.concatenate(
        [pick(left[:E], state), pick(jnp.logical_not(left[:E]), state)], axis=0
    )


def own_state_kernel(len_ref, k_ref, v_ref, state_ref):
    base = lax.axis_index("ctx") * BLK
    _, _, after = block_masks(bounds(len_ref), base)
    left = halves()
    for p in range(PAIRS):
        lanes = slice(p * PAIR, (p + 1) * PAIR)
        k = pick(after, k_ref[0, :, lanes])
        full = dot_tn(k, v_ref[0, :, lanes])
        state_ref[p * E : (p + 1) * E, :] = squeeze_state(left, full).astype(bf16)


def keeps(len_ref):
    begins = bounds(len_ref)
    out = []
    for j in range(NBLK):
        opened = jnp.bool_(False)
        for begin in begins:
            opened = jnp.logical_or(
                opened, jnp.logical_and(begin >= j * BLK, begin < (j + 1) * BLK)
            )
        out.append(jnp.where(opened, 0.0, 1.0).astype(f32))
    return out


def scan_kernel(len_ref, x_ref, o_ref):
    keep = keeps(len_ref)
    carry = jnp.zeros((ROWS, PAIR), f32)
    for j in range(NBLK):
        o_ref[j] = carry.astype(bf16)
        carry = x_ref[j].astype(f32) + keep[j] * carry


def back_scan_kernel(len_ref, x_ref, o_ref):
    keep = keeps(len_ref)
    carry = jnp.zeros((ROWS, PAIR), f32)
    gain = jnp.zeros((1, PAIR), f32)
    for j in reversed(range(NBLK)):
        o_ref[j, :ROWS] = carry.astype(bf16)
        carry = x_ref[j, :ROWS].astype(f32) + keep[j] * carry
        gain = gain + x_ref[j, ROWS : ROWS + 1].astype(f32) + x_ref[j, ROWS + 1 : ROWS + 2].astype(f32)
    high = gain.astype(bf16)
    low = (gain - high.astype(f32)).astype(bf16)
    tile = jnp.concatenate([high, low, jnp.zeros((WIDE - ROWS - 2, PAIR), bf16)], axis=0)
    for j in range(NBLK):
        o_ref[j, ROWS:] = tile


def middle_kernel(
    len_ref, q_ref, k_ref, v_ref, g_ref, gain_ref, c_ref, out_ref, gq_ref, pk_ref, pv_ref, back_ref
):
    base = lax.axis_index("ctx") * BLK
    doc_mask, before, _ = block_masks(bounds(len_ref), base)
    mask2 = jnp.concatenate([doc_mask, doc_mask], axis=0)
    left = halves()
    same = (lax.broadcasted_iota(jnp.int32, (PAIR, PAIR), 0) < E) == left
    ones = jnp.where(same, 1.0 / E, 0.0).astype(bf16)
    ones2 = jnp.concatenate([ones, ones], axis=0)
    for p in range(PAIRS):
        lanes = slice(p * PAIR, (p + 1) * PAIR)
        q, k, v = q_ref[0, :, lanes], k_ref[0, :, lanes], v_ref[0, :, lanes]
        gain = gain_ref[:, lanes]
        q2, k2, v2 = heads(left, q), heads(left, k), heads(left, v)
        carried = spread_state(left, c_ref[p * E : (p + 1) * E, :])
        qb = pick(before, q)
        weights = pick(mask2, dot_nt(q2, k)).astype(bf16)
        att = dot(jnp.concatenate([weights[:BLK], weights[BLK:]], axis=1), v2) + dot(qb, carried)
        dy = g_ref[0, :, lanes].astype(f32)
        d = dy * gain
        terms = jnp.concatenate([att * att, d * att], axis=0)
        high = terms.astype(bf16)
        low = (terms - high.astype(f32)).astype(bf16)
        means = dot(jnp.concatenate([high, low], axis=1), ones2)
        r = lax.rsqrt(means[:BLK] + eps)
        normed = att * r
        out_ref[0, :, lanes] = (gain * normed).astype(bf16)
        ga = ((d - normed * (means[BLK:] * r)) * r).astype(bf16)
        part = jnp.sum(dy * normed, axis=0, keepdims=True)
        part_high = part.astype(bf16)
        part_low = (part - part_high.astype(f32)).astype(bf16)
        tile = jnp.concatenate(
            [part_high, part_low, jnp.zeros((WIDE - ROWS - 2, PAIR), bf16)], axis=0
        )
        state = squeeze_state(left, dot_tn(qb, ga)).astype(bf16)
        for i in range(2):
            back_ref[2 * p + i, :ROWS] = state[i * ROWS : (i + 1) * ROWS]
            back_ref[2 * p + i, ROWS:] = tile
        ga2 = heads(left, ga)
        gw = pick(mask2, dot_nt(ga2, v)).astype(bf16)
        gq = dot(jnp.concatenate([gw[:BLK], gw[BLK:]], axis=1), k2)
        gq = gq + dot_nt(pick(before, ga), carried)
        gq_ref[0, :, lanes] = gq.astype(bf16)
        pk_ref[:, lanes] = dot_tn(gw, q2)
        pv_ref[:, lanes] = dot_tn(weights, ga2)


def last_kernel(len_ref, k_ref, v_ref, pk_ref, pv_ref, bc_ref, gk_ref, gv_ref, gain_ref):
    base = lax.axis_index("ctx") * BLK
    _, _, after = block_masks(bounds(len_ref), base)
    left = halves()
    for p in range(PAIRS):
        lanes = slice(p * PAIR, (p + 1) * PAIR)
        k = pick(after, k_ref[0, :, lanes])
        v = pick(after, v_ref[0, :, lanes])
        state = jnp.concatenate([bc_ref[2 * p, :ROWS], bc_ref[2 * p + 1, :ROWS]], axis=0)
        carried = spread_state(left, state)
        gk_ref[0, :, lanes] = (pk_ref[:, lanes] + dot_nt(v, carried)).astype(bf16)
        gv_ref[0, :, lanes] = (pv_ref[:, lanes] + dot(k, carried)).astype(bf16)
        high = bc_ref[2 * p, ROWS : ROWS + 1].astype(f32)
        gain_ref[:, lanes] = high + bc_ref[2 * p, ROWS + 1 : ROWS + 2].astype(f32)


def call(kernel, outs, n_in, name):
    vmem = pl.BlockSpec(memory_space=pltpu.VMEM)
    smem = pl.BlockSpec(memory_space=pltpu.SMEM)
    return pl.pallas_call(
        kernel,
        out_shape=outs,
        in_specs=[smem] + [vmem] * n_in,
        out_specs=jax.tree.map(lambda _: vmem, outs),
        compiler_params=pltpu.CompilerParams(vmem_limit_bytes=48 << 20),
        name=name,
    )


def per_device(queries, keys, values, grad_output, out_gain, doc_lengths):
    shape = jax.ShapeDtypeStruct
    full = shape(queries.shape, bf16)
    plain = shape((BLK, H * E), f32)
    narrow = shape((NBLK, ROWS, PAIR), bf16)
    wide = shape((NBLK, WIDE, PAIR), bf16)
    gain = out_gain.reshape(1, H * E)

    def swap(a):
        return lax.all_to_all(a, "ctx", 0, 0, tiled=True)

    own = call(own_state_kernel, shape((PAIRS * E, PAIR), bf16), 2, "own_state")(
        doc_lengths, keys, values
    )
    moved = swap(own.reshape(narrow.shape))
    moved = call(scan_kernel, narrow, 1, "scan")(doc_lengths, moved)
    carried = swap(moved).reshape(PAIRS * E, PAIR)
    output, grad_q, part_k, part_v, back = call(
        middle_kernel, (full, full, plain, plain, wide), 6, "middle"
    )(doc_lengths, queries, keys, values, grad_output, gain, carried)
    moved = swap(back)
    moved = call(back_scan_kernel, wide, 1, "back_scan")(doc_lengths, moved)
    back_carried = swap(moved)
    grad_k, grad_v, gain_terms = call(last_kernel, (full, full, shape((1, H * E), f32)), 5, "last")(
        doc_lengths, keys, values, part_k, part_v, back_carried
    )
    total_tokens = lax.axis_size("dp") * BLK * lax.axis_size("ctx")
    grad_gain = lax.psum(gain_terms.reshape(H * E), "dp") / math.sqrt(total_tokens)
    return (output, grad_q, grad_k, grad_v, grad_gain)


def solution(mesh):
    split = P("dp", "ctx", None)
    return jax.shard_map(
        per_device,
        mesh=mesh,
        in_specs=(split, split, split, split, P(), P("dp", None)),
        out_specs=(split, split, split, split, P()),
        check_vma=False,
    )
```

```python
import math

import jax
import jax.numpy as jnp
from jax import lax
from jax.experimental import pallas as pl
from jax.experimental.pallas import tpu as pltpu
from jax.sharding import PartitionSpec as P

H = 32
E = 64
PAIR = 2 * E
PAIRS = H // 2
HALF = PAIRS // 2
DOCS = 12
BLK = 128
CORES = 2
NX = 4
NY = 4
ROWS = HALF * E
SLICE = ROWS // NX
TILE = 2 * PAIRS

eps = 1e-05
f32 = jnp.float32
bf16 = jnp.bfloat16
i32 = jnp.int32


def dot(a, b):
    return lax.dot_general(a, b, (((1,), (0,)), ((), ())), preferred_element_type=f32)


def dot_nt(a, b):
    return lax.dot_general(a, b, (((1,), (1,)), ((), ())), preferred_element_type=f32)


def dot_tn(a, b):
    return lax.dot_general(a, b, (((0,), (0,)), ((), ())), preferred_element_type=f32)


def place():
    index = lax.axis_index("ctx")
    chip = index // CORES
    return index % CORES, chip % NX, chip // NX, chip


def bounds(len_ref):
    begins, total = [], jnp.int32(0)
    for k in range(DOCS):
        begins.append(total)
        total = total + len_ref[0, k]
    return begins


def clear(begins, low, size):
    found = jnp.bool_(False)
    for begin in begins:
        found = jnp.logical_or(found, jnp.logical_and(begin >= low, begin < low + size))
    return jnp.where(found, 0.0, 1.0).astype(f32)


def doc_ids(begins, positions):
    ids = jnp.zeros(positions.shape, i32)
    for begin in begins:
        ids = ids + (positions >= begin).astype(i32)
    return ids


def started(begins, end):
    count = jnp.int32(0)
    for begin in begins:
        count = count + (begin < end).astype(i32)
    return count


def positions(dim):
    return lax.broadcasted_iota(i32, (BLK, BLK), dim) + lax.axis_index("ctx") * BLK


def before_mask(begins):
    return doc_ids(begins, positions(0)) == started(begins, lax.axis_index("ctx") * BLK)


def after_mask(begins):
    return doc_ids(begins, positions(0)) == started(begins, (lax.axis_index("ctx") + 1) * BLK)


def pair_mask(begins):
    row, col = positions(0), positions(1)
    mask = jnp.logical_and(row >= col, doc_ids(begins, row) == doc_ids(begins, col))
    return jnp.concatenate([mask, mask], axis=0)


def left_lanes(rows):
    return lax.broadcasted_iota(i32, (rows, PAIR), 1) < E


def pick(cond, a):
    return jnp.where(cond, a, jnp.zeros_like(a))


def heads(a):
    left = left_lanes(a.shape[0])
    return jnp.concatenate([pick(left, a), pick(jnp.logical_not(left), a)], axis=0)


def fold(full):
    return jnp.where(left_lanes(E), full[:E], full[E:])


def beside(a):
    return jnp.concatenate([a[:BLK], a[BLK:]], axis=1)


def split(a):
    high = a.astype(bf16)
    return high, (a - high.astype(f32)).astype(bf16)


def local_pairs(core):
    for i in range(PAIRS):
        pair = (core * HALF + i) % PAIRS
        yield i, pair, pl.ds(pl.multiple_of(pair * PAIR, PAIR), PAIR)


def own_state_kernel(len_ref, k_ref, v_ref, keep_ref, send_ref):
    core, _, _, _ = place()
    after = after_mask(bounds(len_ref))
    for i, _, lanes in local_pairs(core):
        k = pick(after, k_ref[0, :, lanes])
        state = fold(dot_tn(k, v_ref[0, :, lanes])).astype(bf16)
        ref = keep_ref if i < HALF else send_ref
        ref[i % HALF * E : (i % HALF + 1) * E, :] = state


def rows_of(s):
    return pl.ds(pl.multiple_of(s * SLICE, SLICE), SLICE)


def chip_kernel(back):
    def kernel(len_ref, keep_ref, got_ref, *refs):
        core, x, _, chip = place()
        begins = bounds(len_ref)
        if back:
            gain_ref, *outs = refs
            high, low = split(gain_ref[...])
            gain = high.astype(f32) + low.astype(f32)
            gain = gain + (
                got_ref[ROWS : ROWS + PAIRS].astype(f32) + got_ref[ROWS + PAIRS :].astype(f32)
            )
            tile = jnp.concatenate(split(gain), axis=0)
        else:
            outs = refs
        through = clear(begins, (CORES * chip + (0 if back else 1)) * BLK, BLK)
        mine_passes = (core == 1) if back else (core == 0)
        a = jnp.where(mine_passes, through, 1.0)
        b = jnp.where(mine_passes, 1.0, through)
        for o, out in enumerate(outs):
            rows = rows_of((x + o) % NX)
            total = a * keep_ref[rows, :].astype(f32) + b * got_ref[rows, :].astype(f32)
            out[:SLICE] = total.astype(bf16)
            if back:
                out[SLICE:] = tile

    return kernel


def chips(refs, scratch, x):
    for o, ref in enumerate(refs):
        scratch[(x - o) % NX] = ref[...]
    return scratch


def chip_keeps(begins, y):
    return [clear(begins, (NX * y + xx) * CORES * BLK, CORES * BLK) for xx in range(NX)]


def row_kernel(back):
    def kernel(len_ref, r0, r1, r2, r3, out_ref, scratch):
        _, x, y, _ = place()
        keep = chip_keeps(bounds(len_ref), y)
        totals = chips((r0, r1, r2, r3), scratch, x)
        order = range(NX - 1, -1, -1) if back else range(NX)
        row = jnp.zeros((SLICE, PAIR), f32)
        for xx in order:
            row = totals[xx, :SLICE].astype(f32) + keep[xx] * row
        out_ref[:SLICE] = row.astype(bf16)
        if back:
            gain = jnp.zeros((PAIRS, PAIR), f32)
            for xx in range(NX):
                gain = gain + (
                    totals[xx, SLICE : SLICE + PAIRS].astype(f32)
                    + totals[xx, SLICE + PAIRS :].astype(f32)
                )
            out_ref[SLICE:] = jnp.concatenate(split(gain), axis=0)

    return kernel


def carry_kernel(back):
    def kernel(len_ref, r0, r1, r2, r3, a1_ref, a2_ref, *refs):
        _, x, y, _ = place()
        begins = bounds(len_ref)
        keep = chip_keeps(begins, y)
        if back:
            own_ref, a3_ref, o0, o1, o2, o3, gain_ref, scratch, moved, rows = refs
        else:
            o0, o1, o2, o3, scratch, moved = refs
        totals = chips((r0, r1, r2, r3), scratch, x)
        near = (y < NY - 1) if back else (y > 0)
        far = (y < NY - 2) if back else (y > 1)
        between = clear(begins, (y + (1 if back else -1)) * NX * CORES * BLK, NX * CORES * BLK)
        carry = jnp.where(near, 1.0, 0.0) * a1_ref[:SLICE].astype(f32)
        carry = carry + jnp.where(far, between, 0.0) * a2_ref[:SLICE].astype(f32)
        for xx in range(NX - 1, -1, -1) if back else range(NX):
            moved[xx] = carry.astype(bf16)
            carry = totals[xx, :SLICE].astype(f32) + keep[xx] * carry
        for o, out in enumerate((o0, o1, o2, o3)):
            out[...] = moved[(x + o) % NX]
        if back:
            parts = (own_ref[SLICE:], a1_ref[SLICE:], a2_ref[SLICE:], a3_ref[...])
            for o, part in enumerate(parts):
                rows[(y + o) % NY] = part[:PAIRS].astype(f32) + part[PAIRS:].astype(f32)
            gain_ref[...] = (rows[0] + rows[1]) + (rows[2] + rows[3])

    return kernel


def spread_kernel(back):
    def kernel(len_ref, d0, d1, d2, d3, keep_ref, got_ref, mine_ref, send_ref):
        core, x, _, chip = place()
        first = 1 if back else 0
        keep = clear(bounds(len_ref), (CORES * chip + first) * BLK, BLK)
        is_first = core == first
        for o, ref in enumerate((d0, d1, d2, d3)):
            rows = rows_of((x - o) % NX)
            state = jnp.where(is_first, keep_ref[rows, :].astype(f32), got_ref[rows, :].astype(f32))
            c = ref[...].astype(f32)
            d = state + keep * c
            mine_ref[rows, :] = jnp.where(is_first, c, d).astype(bf16)
            send_ref[rows, :] = jnp.where(is_first, d, c).astype(bf16)

    return kernel


def state_of(i, mine_ref, other_ref):
    ref = mine_ref if i < HALF else other_ref
    return heads(ref[i % HALF * E : (i % HALF + 1) * E, :])


def inside_kernel(len_ref, q_ref, k_ref, v_ref, w_ref, att_ref):
    mask = pair_mask(bounds(len_ref))
    for p in range(PAIRS):
        lanes = slice(p * PAIR, (p + 1) * PAIR)
        q2 = heads(q_ref[0, :, lanes])
        weights = pick(mask, dot_nt(q2, k_ref[0, :, lanes])).astype(bf16)
        w_ref[p] = weights
        att_ref[:, lanes] = dot(beside(weights), heads(v_ref[0, :, lanes]))


def attend_kernel(
    len_ref, q_ref, g_ref, gain_ref, att_ref, mine_ref, other_ref,
    out_ref, ga_ref, keep_ref, send_ref, part_ref,
):
    core, _, _, _ = place()
    before = before_mask(bounds(len_ref))
    same = (lax.broadcasted_iota(i32, (PAIR, PAIR), 0) < E) == left_lanes(PAIR)
    ones = jnp.where(same, 1.0 / E, 0.0).astype(bf16)
    ones2 = jnp.concatenate([ones, ones], axis=0)
    for i, pair, lanes in local_pairs(core):
        gain = gain_ref[:, lanes]
        qb = pick(before, q_ref[0, :, lanes])
        att = att_ref[:, lanes] + dot(qb, state_of(i, mine_ref, other_ref))
        dy = g_ref[0, :, lanes].astype(f32)
        d = dy * gain
        means = dot(
            jnp.concatenate(split(jnp.concatenate([att * att, d * att], axis=0)), axis=1), ones2
        )
        r = lax.rsqrt(means[:BLK] + eps)
        normed = att * r
        out_ref[0, :, lanes] = (gain * normed).astype(bf16)
        ga = ((d - normed * (means[BLK:] * r)) * r).astype(bf16)
        ga_ref[:, lanes] = ga
        part_ref[pl.ds(pair, 1), :] = jnp.sum(dy * normed, axis=0, keepdims=True)
        ref = keep_ref if i < HALF else send_ref
        ref[i % HALF * E : (i % HALF + 1) * E, :] = fold(dot_tn(qb, ga)).astype(bf16)
    high, low = split(part_ref[...])
    send_ref[ROWS : ROWS + PAIRS] = high
    send_ref[ROWS + PAIRS :] = low


def grads_kernel(
    len_ref, q_ref, k_ref, v_ref, w_ref, ga_ref, mine_ref, other_ref, gq_ref, pk_ref, pv_ref
):
    core, _, _, _ = place()
    begins = bounds(len_ref)
    mask, before = pair_mask(begins), before_mask(begins)
    for i, pair, lanes in local_pairs(core):
        ga = ga_ref[:, lanes]
        ga2 = heads(ga)
        gw = pick(mask, dot_nt(ga2, v_ref[0, :, lanes])).astype(bf16)
        gq = dot(beside(gw), heads(k_ref[0, :, lanes]))
        gq = gq + dot_nt(pick(before, ga), state_of(i, mine_ref, other_ref))
        gq_ref[0, :, lanes] = gq.astype(bf16)
        pk_ref[:, lanes] = dot_tn(gw, heads(q_ref[0, :, lanes]))
        pv_ref[:, lanes] = dot_tn(w_ref[pair], ga2)


def last_kernel(
    len_ref, k_ref, v_ref, pk_ref, pv_ref, mine_ref, other_ref, gk_ref, gv_ref
):
    core, _, _, _ = place()
    after = after_mask(bounds(len_ref))
    for i, _, lanes in local_pairs(core):
        k = pick(after, k_ref[0, :, lanes])
        v = pick(after, v_ref[0, :, lanes])
        carried = state_of(i, mine_ref, other_ref)
        gk_ref[0, :, lanes] = (pk_ref[:, lanes] + dot_nt(v, carried)).astype(bf16)
        gv_ref[0, :, lanes] = (pv_ref[:, lanes] + dot(k, carried)).astype(bf16)


def call(kernel, outs, n_in, name, scratch=()):
    vmem = pl.BlockSpec(memory_space=pltpu.VMEM)
    smem = pl.BlockSpec(memory_space=pltpu.SMEM)
    return pl.pallas_call(
        kernel,
        out_shape=outs,
        in_specs=[smem] + [vmem] * n_in,
        out_specs=jax.tree.map(lambda _: vmem, outs),
        scratch_shapes=list(scratch),
        compiler_params=pltpu.CompilerParams(vmem_limit_bytes=48 << 20),
        name=name,
    )


def moves(to):
    pairs = []
    for y in range(NY):
        for x in range(NX):
            for core in range(CORES):
                y2, x2, core2 = to(y, x, core)
                pairs.append(
                    ((y * NX + x) * CORES + core, (y2 % NY * NX + x2 % NX) * CORES + core2)
                )
    return pairs


def across(a):
    return lax.ppermute(a, "ctx", moves(lambda y, x, core: (y, x, 1 - core)))


def along_x(arrays):
    return [arrays[0]] + [
        lax.ppermute(arrays[o], "ctx", moves(lambda y, x, core: (y, x + o, core)))
        for o in range(1, NX)
    ]


def along_y(a, o):
    return lax.ppermute(a, "ctx", moves(lambda y, x, core: (y + o, x, core)))


def chain(lengths, keep, send, back, part=None):
    shape = jax.ShapeDtypeStruct
    rows = SLICE + TILE if back else SLICE
    wide, narrow = shape((rows, PAIR), bf16), shape((SLICE, PAIR), bf16)
    half = shape((ROWS, PAIR), bf16)
    name = "back" if back else "ahead"
    stage = pltpu.VMEM((NX, rows, PAIR), bf16)
    moved = pltpu.VMEM((NX, SLICE, PAIR), bf16)
    got = across(send)
    extra = (part,) if back else ()
    totals = call(chip_kernel(back), (wide,) * NX, 2 + len(extra), name + "_chip")(
        lengths, keep, got, *extra
    )
    totals = along_x(totals)
    row = call(row_kernel(back), wide, NX, name + "_row", [stage])(lengths, *totals)
    step = -1 if back else 1
    near, far = along_y(row, step), along_y(row, 2 * step)
    gains = None
    if back:
        rest = along_y(row[SLICE:], 3 * step)
        *out, gains = call(
            carry_kernel(back),
            (narrow,) * NX + (shape((PAIRS, PAIR), f32),),
            NX + 4,
            name + "_carry",
            [stage, moved, pltpu.VMEM((NY, PAIRS, PAIR), f32)],
        )(lengths, *totals, near, far, row, rest)
    else:
        out = call(carry_kernel(back), (narrow,) * NX, NX + 2, name + "_carry", [stage, moved])(
            lengths, *totals, near, far
        )
    out = along_x(out)
    mine, other = call(spread_kernel(back), (half, half), NX + 2, name + "_spread")(
        lengths, *out, keep, got
    )
    return mine, across(other), gains


def over_dp(gains):
    count = lax.axis_size("dp")
    step = 1
    while step < count:
        gains = gains + lax.ppermute(gains, "dp", [(i, i ^ step) for i in range(count)])
        step *= 2
    return gains


def per_device(queries, keys, values, grad_output, out_gain, doc_lengths):
    shape = jax.ShapeDtypeStruct
    full = shape(queries.shape, bf16)
    plain = shape((BLK, H * E), f32)
    half = shape((ROWS, PAIR), bf16)
    gain = out_gain.reshape(1, H * E)
    keep, send = call(own_state_kernel, (half, half), 2, "own_state")(doc_lengths, keys, values)
    weights, inside = call(
        inside_kernel, (shape((PAIRS, 2 * BLK, BLK), bf16), plain), 3, "inside"
    )(doc_lengths, queries, keys, values)
    mine, other, _ = chain(doc_lengths, keep, send, False)
    output, grad_att, keep, send, part = call(
        attend_kernel,
        (
            full,
            shape((BLK, H * E), bf16),
            half,
            shape((ROWS + TILE, PAIR), bf16),
            shape((PAIRS, PAIR), f32),
        ),
        6,
        "attend",
    )(doc_lengths, queries, grad_output, gain, inside, mine, other)
    grad_q, part_k, part_v = call(grads_kernel, (full, plain, plain), 7, "grads")(
        doc_lengths, queries, keys, values, weights, grad_att, mine, other
    )
    mine, other, gains = chain(doc_lengths, keep, send, True, part)
    grad_k, grad_v = call(last_kernel, (full, full), 6, "last")(
        doc_lengths, keys, values, part_k, part_v, mine, other
    )
    total_tokens = lax.axis_size("dp") * BLK * lax.axis_size("ctx")
    grad_gain = over_dp(gains).reshape(H * E) / math.sqrt(total_tokens)
    return (output, grad_q, grad_k, grad_v, grad_gain)


def solution(mesh):
    spread = P("dp", "ctx", None)
    return jax.shard_map(
        per_device,
        mesh=mesh,
        in_specs=(spread, spread, spread, spread, P(), P("dp", None)),
        out_specs=(spread, spread, spread, spread, P()),
        check_vma=False,
    )
```

```python
import math

import jax
import jax.numpy as jnp
from jax import lax
from jax.experimental import pallas as pl
from jax.experimental.pallas import tpu as pltpu
from jax.sharding import PartitionSpec as P

H = 32
E = 64
PAIR = 2 * E
PAIRS = H // 2
DOCS = 12
BLK = 128
GROUP = 4
SHARE = PAIRS // GROUP
ROWS = SHARE * E
TILE = 2 * PAIRS
REACH = 3

eps = 1e-05
f32 = jnp.float32
bf16 = jnp.bfloat16
i32 = jnp.int32


def dot(a, b):
    return lax.dot_general(a, b, (((1,), (0,)), ((), ())), preferred_element_type=f32)


def dot_nt(a, b):
    return lax.dot_general(a, b, (((1,), (1,)), ((), ())), preferred_element_type=f32)


def dot_tn(a, b):
    return lax.dot_general(a, b, (((0,), (0,)), ((), ())), preferred_element_type=f32)


def place():
    index = lax.axis_index("ctx")
    return index % GROUP, index // GROUP


def bounds(len_ref):
    begins, total = [], jnp.int32(0)
    for k in range(DOCS):
        begins.append(total)
        total = total + len_ref[0, k]
    return begins


def clear(begins, low, size):
    found = jnp.bool_(False)
    for begin in begins:
        found = jnp.logical_or(found, jnp.logical_and(begin >= low, begin < low + size))
    return jnp.where(found, 0.0, 1.0).astype(f32)


def doc_ids(begins, positions):
    ids = jnp.zeros(positions.shape, i32)
    for begin in begins:
        ids = ids + (positions >= begin).astype(i32)
    return ids


def started(begins, end):
    count = jnp.int32(0)
    for begin in begins:
        count = count + (begin < end).astype(i32)
    return count


def positions(dim):
    return lax.broadcasted_iota(i32, (BLK, BLK), dim) + lax.axis_index("ctx") * BLK


def before_mask(begins):
    return doc_ids(begins, positions(0)) == started(begins, lax.axis_index("ctx") * BLK)


def after_mask(begins):
    return doc_ids(begins, positions(0)) == started(begins, (lax.axis_index("ctx") + 1) * BLK)


def pair_mask(begins):
    row, col = positions(0), positions(1)
    mask = jnp.logical_and(row >= col, doc_ids(begins, row) == doc_ids(begins, col))
    return jnp.concatenate([mask, mask], axis=0)


def left_lanes(rows):
    return lax.broadcasted_iota(i32, (rows, PAIR), 1) < E


def pick(cond, a):
    return jnp.where(cond, a, jnp.zeros_like(a))


def heads(a):
    left = left_lanes(a.shape[0])
    return jnp.concatenate([pick(left, a), pick(jnp.logical_not(left), a)], axis=0)


def fold(full):
    return jnp.where(left_lanes(E), full[:E], full[E:])


def beside(a):
    return jnp.concatenate([a[:BLK], a[BLK:]], axis=1)


def split(a):
    high = a.astype(bf16)
    return high, (a - high.astype(f32)).astype(bf16)


def local_pairs(r):
    for o in range(GROUP):
        for i in range(SHARE):
            pair = (r ^ o) * SHARE + i
            yield o, slice(i * E, (i + 1) * E), pair, pl.ds(pl.multiple_of(pair * PAIR, PAIR), PAIR)


def own_state_kernel(len_ref, k_ref, v_ref, *state_refs):
    r, _ = place()
    after = after_mask(bounds(len_ref))
    for o, rows, _, lanes in local_pairs(r):
        k = pick(after, k_ref[0, :, lanes])
        state_refs[o][rows, :] = fold(dot_tn(k, v_ref[0, :, lanes])).astype(bf16)


def block_keeps(begins, group):
    return [clear(begins, (group * GROUP + b) * BLK, BLK) for b in range(GROUP)]


def order(back):
    return range(GROUP - 1, -1, -1) if back else range(GROUP)


def joined(tile):
    return tile[:PAIRS].astype(f32) + tile[PAIRS:].astype(f32)


def total_kernel(back):
    def kernel(len_ref, *refs):
        r, group = place()
        states = refs[:GROUP]
        if back:
            part_ref, out_ref, gain_ref, scratch = refs[GROUP:]
        else:
            out_ref, scratch = refs[GROUP:]
        keep = block_keeps(bounds(len_ref), group)
        for o, ref in enumerate(states):
            scratch[r ^ o] = ref[:ROWS]
        total = scratch[order(back)[0]].astype(f32)
        for b in order(back)[1:]:
            total = scratch[b].astype(f32) + keep[b] * total
        out_ref[...] = total.astype(bf16)
        if back:
            high, low = split(part_ref[...])
            own = high.astype(f32) + low.astype(f32)
            g1, g2, g3 = (joined(ref[ROWS:]) for ref in states[1:])
            gain_ref[...] = (own + g1) + (g2 + g3)

    return kernel


def carry_kernel(back):
    def kernel(len_ref, *refs):
        r, group = place()
        begins = bounds(len_ref)
        states, far, outs = refs[:GROUP], refs[GROUP : GROUP + REACH], refs[GROUP + REACH : -2]
        scratch, moved = refs[-2:]
        keep = block_keeps(begins, group)
        for o, ref in enumerate(states):
            scratch[r ^ o] = ref[:ROWS]
        carry = jnp.zeros((ROWS, PAIR), f32)
        for d in range(REACH, 0, -1):
            source = group + d if back else group - d
            inside = (source < lax.axis_size("ctx") // GROUP) if back else (source >= 0)
            through = clear(begins, source * GROUP * BLK, GROUP * BLK)
            carry = through * carry + jnp.where(inside, 1.0, 0.0) * far[d - 1][...].astype(f32)
        for b in order(back):
            moved[b] = carry.astype(bf16)
            carry = scratch[b].astype(f32) + keep[b] * carry
        for o, out in enumerate(outs):
            out[...] = moved[r ^ o]

    return kernel


def inside_kernel(len_ref, q_ref, k_ref, v_ref, w_ref, att_ref):
    mask = pair_mask(bounds(len_ref))
    for p in range(PAIRS):
        lanes = slice(p * PAIR, (p + 1) * PAIR)
        q2 = heads(q_ref[0, :, lanes])
        weights = pick(mask, dot_nt(q2, k_ref[0, :, lanes])).astype(bf16)
        w_ref[p] = weights
        att_ref[:, lanes] = dot(beside(weights), heads(v_ref[0, :, lanes]))


def attend_kernel(len_ref, q_ref, g_ref, gain_ref, att_ref, *refs):
    c_refs, (out_ref, ga_ref), state_refs = refs[:GROUP], refs[GROUP : GROUP + 2], refs[GROUP + 2 : -1]
    part_ref = refs[-1]
    r, _ = place()
    before = before_mask(bounds(len_ref))
    same = (lax.broadcasted_iota(i32, (PAIR, PAIR), 0) < E) == left_lanes(PAIR)
    ones = jnp.where(same, 1.0 / E, 0.0).astype(bf16)
    ones2 = jnp.concatenate([ones, ones], axis=0)
    for o, rows, pair, lanes in local_pairs(r):
        gain = gain_ref[:, lanes]
        qb = pick(before, q_ref[0, :, lanes])
        att = att_ref[:, lanes] + dot(qb, heads(c_refs[o][rows, :]))
        dy = g_ref[0, :, lanes].astype(f32)
        d = dy * gain
        means = dot(
            jnp.concatenate(split(jnp.concatenate([att * att, d * att], axis=0)), axis=1), ones2
        )
        root = lax.rsqrt(means[:BLK] + eps)
        normed = att * root
        out_ref[0, :, lanes] = (gain * normed).astype(bf16)
        ga = ((d - normed * (means[BLK:] * root)) * root).astype(bf16)
        ga_ref[:, lanes] = ga
        part_ref[pl.ds(pair, 1), :] = jnp.sum(dy * normed, axis=0, keepdims=True)
        state_refs[o][rows, :] = fold(dot_tn(qb, ga)).astype(bf16)
    tile = jnp.concatenate(split(part_ref[...]), axis=0)
    for ref in state_refs[1:]:
        ref[ROWS:] = tile


def grads_kernel(len_ref, q_ref, k_ref, v_ref, w_ref, ga_ref, *refs):
    c_refs, (gq_ref, pk_ref, pv_ref) = refs[:GROUP], refs[GROUP:]
    r, _ = place()
    begins = bounds(len_ref)
    mask, before = pair_mask(begins), before_mask(begins)
    for o, rows, pair, lanes in local_pairs(r):
        ga = ga_ref[:, lanes]
        ga2 = heads(ga)
        gw = pick(mask, dot_nt(ga2, v_ref[0, :, lanes])).astype(bf16)
        gq = dot(beside(gw), heads(k_ref[0, :, lanes]))
        gq = gq + dot_nt(pick(before, ga), heads(c_refs[o][rows, :]))
        gq_ref[0, :, lanes] = gq.astype(bf16)
        pk_ref[:, lanes] = dot_tn(gw, heads(q_ref[0, :, lanes]))
        pv_ref[:, lanes] = dot_tn(w_ref[pair], ga2)


def last_kernel(len_ref, k_ref, v_ref, pk_ref, pv_ref, *refs):
    c_refs, (gk_ref, gv_ref) = refs[:GROUP], refs[GROUP:]
    r, _ = place()
    after = after_mask(bounds(len_ref))
    for o, rows, _, lanes in local_pairs(r):
        k = pick(after, k_ref[0, :, lanes])
        v = pick(after, v_ref[0, :, lanes])
        carried = heads(c_refs[o][rows, :])
        gk_ref[0, :, lanes] = (pk_ref[:, lanes] + dot_nt(v, carried)).astype(bf16)
        gv_ref[0, :, lanes] = (pv_ref[:, lanes] + dot(k, carried)).astype(bf16)


def call(kernel, outs, n_in, name, scratch=()):
    vmem = pl.BlockSpec(memory_space=pltpu.VMEM)
    smem = pl.BlockSpec(memory_space=pltpu.SMEM)
    return pl.pallas_call(
        kernel,
        out_shape=outs,
        in_specs=[smem] + [vmem] * n_in,
        out_specs=jax.tree.map(lambda _: vmem, outs),
        scratch_shapes=list(scratch),
        compiler_params=pltpu.CompilerParams(vmem_limit_bytes=48 << 20),
        name=name,
    )


def exchange(arrays):
    count = lax.axis_size("ctx")
    got = [
        lax.ppermute(arrays[o], "ctx", [(i, i ^ o) for i in range(count)])
        for o in range(GROUP - 1, 0, -1)
    ]
    return [arrays[0]] + got[::-1]


def among(terms, first, second):
    count = lax.axis_size(("dp", "ctx"))
    a, b, c = (
        lax.ppermute(terms, ("dp", "ctx"), [(i, i ^ bits) for i in range(count)])
        for bits in (first, second, first | second)
    )
    return (terms + a) + (b + c)


def chain(lengths, states, back, part=None):
    shape = jax.ShapeDtypeStruct
    share = shape((ROWS, PAIR), bf16)
    terms = shape((PAIRS, PAIR), f32)
    name = "back" if back else "ahead"
    stage = pltpu.VMEM((GROUP, ROWS, PAIR), bf16)
    count = lax.axis_size("ctx")
    states = exchange(states)
    gains = None
    if back:
        total, gains = call(total_kernel(True), (share, terms), GROUP + 1, name + "_total", [stage])(
            lengths, *states, part
        )
    else:
        total = call(total_kernel(False), share, GROUP, name + "_total", [stage])(lengths, *states)
    step = -GROUP if back else GROUP
    far = [
        lax.ppermute(total, "ctx", [(i, (i + d * step) % count) for i in range(count)])
        for d in range(REACH, 0, -1)
    ][::-1]
    if back:
        gains, *far = lax.optimization_barrier((among(gains, 32, 64), *far))
    outs = call(carry_kernel(back), (share,) * GROUP, GROUP + REACH, name + "_carry", [stage, stage])(
        lengths, *states, *far
    )
    carried = exchange(outs)
    if back:
        gains, *carried = lax.optimization_barrier((among(gains, 8, 16), *carried))
    return carried, gains


def per_device(queries, keys, values, grad_output, out_gain, doc_lengths):
    shape = jax.ShapeDtypeStruct
    full = shape(queries.shape, bf16)
    plain = shape((BLK, H * E), f32)
    share = shape((ROWS, PAIR), bf16)
    wide = shape((ROWS + TILE, PAIR), bf16)
    gain = out_gain.reshape(1, H * E)
    states = call(own_state_kernel, (share,) * GROUP, 2, "own_state")(doc_lengths, keys, values)
    weights, inside = call(
        inside_kernel, (shape((PAIRS, 2 * BLK, BLK), bf16), plain), 3, "inside"
    )(doc_lengths, queries, keys, values)
    carried, _ = chain(doc_lengths, states, False)
    output, grad_att, *states, part = call(
        attend_kernel,
        (full, shape((BLK, H * E), bf16), share, wide, wide, wide, shape((PAIRS, PAIR), f32)),
        4 + GROUP,
        "attend",
    )(doc_lengths, queries, grad_output, gain, inside, *carried)
    grad_q, part_k, part_v = call(grads_kernel, (full, plain, plain), 5 + GROUP, "grads")(
        doc_lengths, queries, keys, values, weights, grad_att, *carried
    )
    carried, gains = chain(doc_lengths, states, True, part)
    grad_k, grad_v = call(last_kernel, (full, full), 4 + GROUP, "last")(
        doc_lengths, keys, values, part_k, part_v, *carried
    )
    total_tokens = lax.axis_size("dp") * BLK * lax.axis_size("ctx")
    grad_gain = among(gains, 4, 128).reshape(H * E) / math.sqrt(total_tokens)
    return (output, grad_q, grad_k, grad_v, grad_gain)


def solution(mesh):
    spread = P("dp", "ctx", None)
    return jax.shard_map(
        per_device,
        mesh=mesh,
        in_specs=(spread, spread, spread, spread, P(), P("dp", None)),
        out_specs=(spread, spread, spread, spread, P()),
        check_vma=False,
    )
```

```python
import math

import jax
import jax.numpy as jnp
from jax import lax
from jax.experimental import pallas as pl
from jax.experimental.pallas import tpu as pltpu
from jax.sharding import PartitionSpec as P

H = 32
E = 64
PAIR = 2 * E
PAIRS = H // 2
DOCS = 12
BLK = 128
GROUP = 4
SHARE = PAIRS // GROUP
ROWS = SHARE * E
TILE = 2 * PAIRS
REACH = 3

eps = 1e-05
f32 = jnp.float32
bf16 = jnp.bfloat16
i32 = jnp.int32


def dot(a, b):
    return lax.dot_general(a, b, (((1,), (0,)), ((), ())), preferred_element_type=f32)


def dot_nt(a, b):
    return lax.dot_general(a, b, (((1,), (1,)), ((), ())), preferred_element_type=f32)


def dot_tn(a, b):
    return lax.dot_general(a, b, (((0,), (0,)), ((), ())), preferred_element_type=f32)


def place():
    index = lax.axis_index("ctx")
    return index % GROUP, index // GROUP


def bounds(len_ref):
    begins, total = [], jnp.int32(0)
    for k in range(DOCS):
        begins.append(total)
        total = total + len_ref[0, k]
    return begins


def clear(begins, low, size):
    found = jnp.bool_(False)
    for begin in begins:
        found = jnp.logical_or(found, jnp.logical_and(begin >= low, begin < low + size))
    return jnp.where(found, 0.0, 1.0).astype(f32)


def doc_ids(begins, positions):
    ids = jnp.zeros(positions.shape, i32)
    for begin in begins:
        ids = ids + (positions >= begin).astype(i32)
    return ids


def started(begins, end):
    count = jnp.int32(0)
    for begin in begins:
        count = count + (begin < end).astype(i32)
    return count


def positions(dim):
    return lax.broadcasted_iota(i32, (BLK, BLK), dim) + lax.axis_index("ctx") * BLK


def before_mask(begins):
    return doc_ids(begins, positions(0)) == started(begins, lax.axis_index("ctx") * BLK)


def after_mask(begins):
    return doc_ids(begins, positions(0)) == started(begins, (lax.axis_index("ctx") + 1) * BLK)


def pair_mask(begins):
    row, col = positions(0), positions(1)
    mask = jnp.logical_and(row >= col, doc_ids(begins, row) == doc_ids(begins, col))
    return jnp.concatenate([mask, mask], axis=0)


def left_lanes(rows):
    return lax.broadcasted_iota(i32, (rows, PAIR), 1) < E


def pick(cond, a):
    return jnp.where(cond, a, jnp.zeros_like(a))


def heads(a):
    left = left_lanes(a.shape[0])
    return jnp.concatenate([pick(left, a), pick(jnp.logical_not(left), a)], axis=0)


def fold(full):
    return jnp.where(left_lanes(E), full[:E], full[E:])


def beside(a):
    return jnp.concatenate([a[:BLK], a[BLK:]], axis=1)


def split(a):
    high = a.astype(bf16)
    return high, (a - high.astype(f32)).astype(bf16)


def local_pairs(r):
    for o in range(GROUP):
        for i in range(SHARE):
            pair = (r ^ o) * SHARE + i
            yield o, slice(i * E, (i + 1) * E), pair, pl.ds(pl.multiple_of(pair * PAIR, PAIR), PAIR)


def own_state_kernel(len_ref, k_ref, v_ref, *state_refs):
    r, _ = place()
    after = after_mask(bounds(len_ref))
    for o, rows, _, lanes in local_pairs(r):
        k = pick(after, k_ref[0, :, lanes])
        state_refs[o][rows, :] = fold(dot_tn(k, v_ref[0, :, lanes])).astype(bf16)


def block_keeps(begins, group):
    return [clear(begins, (group * GROUP + b) * BLK, BLK) for b in range(GROUP)]


def order(back):
    return range(GROUP - 1, -1, -1) if back else range(GROUP)


def joined(tile):
    return tile[:PAIRS].astype(f32) + tile[PAIRS:].astype(f32)


def total_kernel(back):
    def kernel(len_ref, *refs):
        r, group = place()
        states = refs[:GROUP]
        if back:
            part_ref, out_ref, scratch = refs[GROUP:]
        else:
            out_ref, scratch = refs[GROUP:]
        keep = block_keeps(bounds(len_ref), group)
        for o, ref in enumerate(states):
            scratch[r ^ o] = ref[:ROWS]
        total = scratch[order(back)[0]].astype(f32)
        for b in order(back)[1:]:
            total = scratch[b].astype(f32) + keep[b] * total
        out_ref[:ROWS] = total.astype(bf16)
        if back:
            high, low = split(part_ref[...])
            own = high.astype(f32) + low.astype(f32)
            g1, g2, g3 = (joined(ref[ROWS:]) for ref in states[1:])
            out_ref[ROWS:] = jnp.concatenate(split((own + g1) + (g2 + g3)), axis=0)

    return kernel


def carry_kernel(back):
    def kernel(len_ref, *refs):
        r, group = place()
        begins = bounds(len_ref)
        states, far, refs = refs[:GROUP], refs[GROUP : GROUP + REACH], refs[GROUP + REACH :]
        if back:
            own_ref, *outs, terms_ref, scratch, moved = refs
            for d, ref in enumerate((own_ref, *far)):
                terms_ref[d * PAIRS : (d + 1) * PAIRS] = joined(ref[ROWS:])
        else:
            *outs, scratch, moved = refs
        keep = block_keeps(begins, group)
        for o, ref in enumerate(states):
            scratch[r ^ o] = ref[:ROWS]
        carry = jnp.zeros((ROWS, PAIR), f32)
        for d in range(REACH, 0, -1):
            source = group + d if back else group - d
            inside = (source < lax.axis_size("ctx") // GROUP) if back else (source >= 0)
            through = clear(begins, source * GROUP * BLK, GROUP * BLK)
            carry = through * carry + jnp.where(inside, 1.0, 0.0) * far[d - 1][:ROWS].astype(f32)
        for b in order(back):
            moved[b] = carry.astype(bf16)
            carry = scratch[b].astype(f32) + keep[b] * carry
        for o, out in enumerate(outs):
            out[...] = moved[r ^ o]

    return kernel


def gather_kernel(_, mine_ref, theirs_ref, out_ref, scratch):
    _, group = place()
    groups = scratch.shape[0]
    for d in range(groups):
        ref = mine_ref if d < GROUP else theirs_ref
        scratch[(group + d) % groups] = ref[d % GROUP * PAIRS : (d % GROUP + 1) * PAIRS]
    total = scratch[0]
    for g in range(1, groups):
        total = total + scratch[g]
    out_ref[...] = total


def inside_kernel(len_ref, q_ref, k_ref, v_ref, w_ref, att_ref):
    mask = pair_mask(bounds(len_ref))
    for p in range(PAIRS):
        lanes = slice(p * PAIR, (p + 1) * PAIR)
        q2 = heads(q_ref[0, :, lanes])
        weights = pick(mask, dot_nt(q2, k_ref[0, :, lanes])).astype(bf16)
        w_ref[p] = weights
        att_ref[:, lanes] = dot(beside(weights), heads(v_ref[0, :, lanes]))


def attend_kernel(len_ref, q_ref, g_ref, gain_ref, att_ref, *refs):
    c_refs, (out_ref, ga_ref), state_refs = refs[:GROUP], refs[GROUP : GROUP + 2], refs[GROUP + 2 : -1]
    part_ref = refs[-1]
    r, _ = place()
    before = before_mask(bounds(len_ref))
    same = (lax.broadcasted_iota(i32, (PAIR, PAIR), 0) < E) == left_lanes(PAIR)
    ones = jnp.where(same, 1.0 / E, 0.0).astype(bf16)
    ones2 = jnp.concatenate([ones, ones], axis=0)
    for o, rows, pair, lanes in local_pairs(r):
        gain = gain_ref[:, lanes]
        qb = pick(before, q_ref[0, :, lanes])
        att = att_ref[:, lanes] + dot(qb, heads(c_refs[o][rows, :]))
        dy = g_ref[0, :, lanes].astype(f32)
        d = dy * gain
        means = dot(
            jnp.concatenate(split(jnp.concatenate([att * att, d * att], axis=0)), axis=1), ones2
        )
        root = lax.rsqrt(means[:BLK] + eps)
        normed = att * root
        out_ref[0, :, lanes] = (gain * normed).astype(bf16)
        ga = ((d - normed * (means[BLK:] * root)) * root).astype(bf16)
        ga_ref[:, lanes] = ga
        part_ref[pl.ds(pair, 1), :] = jnp.sum(dy * normed, axis=0, keepdims=True)
        state_refs[o][rows, :] = fold(dot_tn(qb, ga)).astype(bf16)
    tile = jnp.concatenate(split(part_ref[...]), axis=0)
    for ref in state_refs[1:]:
        ref[ROWS:] = tile


def grads_kernel(len_ref, q_ref, k_ref, v_ref, w_ref, ga_ref, *refs):
    c_refs, (gq_ref, pk_ref, pv_ref) = refs[:GROUP], refs[GROUP:]
    r, _ = place()
    begins = bounds(len_ref)
    mask, before = pair_mask(begins), before_mask(begins)
    for o, rows, pair, lanes in local_pairs(r):
        ga = ga_ref[:, lanes]
        ga2 = heads(ga)
        gw = pick(mask, dot_nt(ga2, v_ref[0, :, lanes])).astype(bf16)
        gq = dot(beside(gw), heads(k_ref[0, :, lanes]))
        gq = gq + dot_nt(pick(before, ga), heads(c_refs[o][rows, :]))
        gq_ref[0, :, lanes] = gq.astype(bf16)
        pk_ref[:, lanes] = dot_tn(gw, heads(q_ref[0, :, lanes]))
        pv_ref[:, lanes] = dot_tn(w_ref[pair], ga2)


def last_kernel(len_ref, k_ref, v_ref, pk_ref, pv_ref, *refs):
    c_refs, (gk_ref, gv_ref) = refs[:GROUP], refs[GROUP:]
    r, _ = place()
    after = after_mask(bounds(len_ref))
    for o, rows, _, lanes in local_pairs(r):
        k = pick(after, k_ref[0, :, lanes])
        v = pick(after, v_ref[0, :, lanes])
        carried = heads(c_refs[o][rows, :])
        gk_ref[0, :, lanes] = (pk_ref[:, lanes] + dot_nt(v, carried)).astype(bf16)
        gv_ref[0, :, lanes] = (pv_ref[:, lanes] + dot(k, carried)).astype(bf16)


def call(kernel, outs, n_in, name, scratch=()):
    vmem = pl.BlockSpec(memory_space=pltpu.VMEM)
    smem = pl.BlockSpec(memory_space=pltpu.SMEM)
    return pl.pallas_call(
        kernel,
        out_shape=outs,
        in_specs=[smem] + [vmem] * n_in,
        out_specs=jax.tree.map(lambda _: vmem, outs),
        scratch_shapes=list(scratch),
        compiler_params=pltpu.CompilerParams(vmem_limit_bytes=48 << 20),
        name=name,
    )


def exchange(arrays):
    count = lax.axis_size("ctx")
    got = [
        lax.ppermute(arrays[o], "ctx", [(i, i ^ o) for i in range(count)])
        for o in range(GROUP - 1, 0, -1)
    ]
    return [arrays[0]] + got[::-1]


def chain(lengths, states, back, part=None, beside=()):
    shape = jax.ShapeDtypeStruct
    share, wide = shape((ROWS, PAIR), bf16), shape((ROWS + TILE, PAIR), bf16)
    terms, four = shape((PAIRS, PAIR), f32), shape((GROUP * PAIRS, PAIR), f32)
    name = "back" if back else "ahead"
    stage = pltpu.VMEM((GROUP, ROWS, PAIR), bf16)
    count = lax.axis_size("ctx")
    states = exchange(states)
    extra = (part,) if back else ()
    total = call(
        total_kernel(back), wide if back else share, GROUP + len(extra), name + "_total", [stage]
    )(lengths, *states, *extra)
    step = -GROUP if back else GROUP
    far = [
        lax.ppermute(total, "ctx", [(i, (i + d * step) % count) for i in range(count)])
        for d in range(REACH, 0, -1)
    ][::-1]
    if not back:
        outs = call(carry_kernel(False), (share,) * GROUP, GROUP + REACH, name + "_carry", [stage] * 2)(
            lengths, *states, *far
        )
        return exchange(outs), None, beside
    far, beside = lax.optimization_barrier((far, beside))
    *outs, mine = call(
        carry_kernel(True), (share,) * GROUP + (four,), GROUP + REACH + 1, name + "_carry", [stage] * 2
    )(lengths, *states, *far, total)
    theirs = lax.ppermute(mine, "ctx", [(i, (i + count // 2) % count) for i in range(count)])
    gains = call(
        gather_kernel, terms, 2, "gather", [pltpu.VMEM((count // GROUP, PAIRS, PAIR), f32)]
    )(lengths, mine, theirs)
    outs = exchange(outs)
    gains, *outs = lax.optimization_barrier((gains, *outs))
    return outs, gains, beside


def over_dp(gains):
    count = lax.axis_size("dp")
    step = 1
    while step < count:
        gains = gains + lax.ppermute(gains, "dp", [(i, i ^ step) for i in range(count)])
        step *= 2
    return gains


def per_device(queries, keys, values, grad_output, out_gain, doc_lengths):
    shape = jax.ShapeDtypeStruct
    full = shape(queries.shape, bf16)
    plain = shape((BLK, H * E), f32)
    share = shape((ROWS, PAIR), bf16)
    wide = shape((ROWS + TILE, PAIR), bf16)
    gain = out_gain.reshape(1, H * E)
    states = call(own_state_kernel, (share,) * GROUP, 2, "own_state")(doc_lengths, keys, values)
    weights, inside = call(
        inside_kernel, (shape((PAIRS, 2 * BLK, BLK), bf16), plain), 3, "inside"
    )(doc_lengths, queries, keys, values)
    carried, _, _ = chain(doc_lengths, states, False)
    output, grad_att, *states, part = call(
        attend_kernel,
        (full, shape((BLK, H * E), bf16), share, wide, wide, wide, shape((PAIRS, PAIR), f32)),
        4 + GROUP,
        "attend",
    )(doc_lengths, queries, grad_output, gain, inside, *carried)
    parts = call(grads_kernel, (full, plain, plain), 5 + GROUP, "grads")(
        doc_lengths, queries, keys, values, weights, grad_att, *carried
    )
    carried, gains, parts = chain(doc_lengths, states, True, part, parts)
    grad_q, part_k, part_v = parts
    grad_k, grad_v = call(last_kernel, (full, full), 4 + GROUP, "last")(
        doc_lengths, keys, values, part_k, part_v, *carried
    )
    total_tokens = lax.axis_size("dp") * BLK * lax.axis_size("ctx")
    grad_gain = over_dp(gains).reshape(H * E) / math.sqrt(total_tokens)
    return (output, grad_q, grad_k, grad_v, grad_gain)


def solution(mesh):
    spread = P("dp", "ctx", None)
    return jax.shard_map(
        per_device,
        mesh=mesh,
        in_specs=(spread, spread, spread, spread, P(), P("dp", None)),
        out_specs=(spread, spread, spread, spread, P()),
        check_vma=False,
    )
```

```python
import math

import jax
import jax.numpy as jnp
from jax import lax
from jax.experimental import pallas as pl
from jax.experimental.pallas import tpu as pltpu
from jax.sharding import PartitionSpec as P

H = 32
E = 64
PAIR = 2 * E
PAIRS = H // 2
DOCS = 12
BLK = 128
GROUP = 4
SHARE = PAIRS // GROUP
ROWS = SHARE * E
TILE = 2 * PAIRS
BATCHED = 4
REACH = 3

eps = 1e-05
f32 = jnp.float32
bf16 = jnp.bfloat16
i32 = jnp.int32


def dot(a, b):
    return lax.dot_general(a, b, (((1,), (0,)), ((), ())), preferred_element_type=f32)


def dot_nt(a, b):
    return lax.dot_general(a, b, (((1,), (1,)), ((), ())), preferred_element_type=f32)


def dot_tn(a, b):
    return lax.dot_general(a, b, (((0,), (0,)), ((), ())), preferred_element_type=f32)


def place():
    index = lax.axis_index("ctx")
    return index % GROUP, index // GROUP


def bounds(len_ref):
    begins, total = [], jnp.int32(0)
    for k in range(DOCS):
        begins.append(total)
        total = total + len_ref[0, k]
    return begins


def clear(begins, low, size):
    found = jnp.bool_(False)
    for begin in begins:
        found = jnp.logical_or(found, jnp.logical_and(begin >= low, begin < low + size))
    return jnp.where(found, 0.0, 1.0).astype(f32)


def doc_ids(begins, positions):
    ids = jnp.zeros(positions.shape, i32)
    for begin in begins:
        ids = ids + (positions >= begin).astype(i32)
    return ids


def started(begins, end):
    count = jnp.int32(0)
    for begin in begins:
        count = count + (begin < end).astype(i32)
    return count


def positions(dim):
    return lax.broadcasted_iota(i32, (BLK, BLK), dim) + lax.axis_index("ctx") * BLK


def before_mask(begins):
    return doc_ids(begins, positions(0)) == started(begins, lax.axis_index("ctx") * BLK)


def after_mask(begins):
    return doc_ids(begins, positions(0)) == started(begins, (lax.axis_index("ctx") + 1) * BLK)


def pair_mask(begins):
    row, col = positions(0), positions(1)
    mask = jnp.logical_and(row >= col, doc_ids(begins, row) == doc_ids(begins, col))
    return jnp.concatenate([mask, mask], axis=0)


def left_lanes(rows):
    return lax.broadcasted_iota(i32, (rows, PAIR), 1) < E


def pick(cond, a):
    return jnp.where(cond, a, jnp.zeros_like(a))


def heads(a):
    left = left_lanes(a.shape[0])
    return jnp.concatenate([pick(left, a), pick(jnp.logical_not(left), a)], axis=0)


def fold(full):
    return jnp.where(left_lanes(E), full[:E], full[E:])


def beside(a):
    return jnp.concatenate([a[:BLK], a[BLK:]], axis=1)


def split(a):
    high = a.astype(bf16)
    return high, (a - high.astype(f32)).astype(bf16)


def local_pairs(r):
    for o in range(GROUP):
        for i in range(SHARE):
            pair = (r ^ o) * SHARE + i
            yield o, slice(i * E, (i + 1) * E), pair, pl.ds(pl.multiple_of(pair * PAIR, PAIR), PAIR)


def own_state_kernel(len_ref, k_ref, v_ref, *state_refs):
    r, _ = place()
    after = after_mask(bounds(len_ref))
    for o, rows, _, lanes in local_pairs(r):
        k = pick(after, k_ref[0, :, lanes])
        state_refs[o][rows, :] = fold(dot_tn(k, v_ref[0, :, lanes])).astype(bf16)


def block_keeps(begins, group):
    return [clear(begins, (group * GROUP + b) * BLK, BLK) for b in range(GROUP)]


def order(back):
    return range(GROUP - 1, -1, -1) if back else range(GROUP)


def joined(tile):
    return tile[:PAIRS].astype(f32) + tile[PAIRS:].astype(f32)


def total_kernel(back):
    def kernel(len_ref, *refs):
        r, group = place()
        states = refs[:GROUP]
        if back:
            part_ref, out_ref, scratch = refs[GROUP:]
        else:
            out_ref, scratch = refs[GROUP:]
        keep = block_keeps(bounds(len_ref), group)
        for o, ref in enumerate(states):
            scratch[r ^ o] = ref[:ROWS]
        total = scratch[order(back)[0]].astype(f32)
        for b in order(back)[1:]:
            total = scratch[b].astype(f32) + keep[b] * total
        out_ref[:ROWS] = total.astype(bf16)
        if back:
            high, low = split(part_ref[...])
            own = high.astype(f32) + low.astype(f32)
            g1, g2, g3 = (joined(ref[ROWS:]) for ref in states[1:])
            out_ref[ROWS:] = jnp.concatenate(split((own + g1) + (g2 + g3)), axis=0)

    return kernel


def carry_kernel(back):
    def kernel(len_ref, *refs):
        r, group = place()
        begins = bounds(len_ref)
        states, far, refs = refs[:GROUP], refs[GROUP : GROUP + REACH], refs[GROUP + REACH :]
        if back:
            own_ref, *outs, terms_ref, scratch, moved = refs
            for d, ref in enumerate((own_ref, *far)):
                terms_ref[d * PAIRS : (d + 1) * PAIRS] = joined(ref[ROWS:])
        else:
            *outs, scratch, moved = refs
        keep = block_keeps(begins, group)
        for o, ref in enumerate(states):
            scratch[r ^ o] = ref[:ROWS]
        carry = jnp.zeros((ROWS, PAIR), f32)
        for d in range(REACH, 0, -1):
            source = group + d if back else group - d
            inside = (source < lax.axis_size("ctx") // GROUP) if back else (source >= 0)
            through = clear(begins, source * GROUP * BLK, GROUP * BLK)
            carry = through * carry + jnp.where(inside, 1.0, 0.0) * far[d - 1][:ROWS].astype(f32)
        for b in order(back):
            moved[b] = carry.astype(bf16)
            carry = scratch[b].astype(f32) + keep[b] * carry
        for o, out in enumerate(outs):
            out[...] = moved[r ^ o]

    return kernel


def gather_kernel(_, mine_ref, theirs_ref, out_ref, scratch):
    _, group = place()
    groups = scratch.shape[0]
    for d in range(groups):
        ref = mine_ref if d < GROUP else theirs_ref
        scratch[(group + d) % groups] = ref[d % GROUP * PAIRS : (d % GROUP + 1) * PAIRS]
    total = scratch[0]
    for g in range(1, groups):
        total = total + scratch[g]
    out_ref[...] = total


def inside_kernel(len_ref, q_ref, k_ref, v_ref, w_ref, att_ref):
    mask = pair_mask(bounds(len_ref))
    for p in range(PAIRS):
        lanes = slice(p * PAIR, (p + 1) * PAIR)
        q2 = heads(q_ref[0, :, lanes])
        weights = pick(mask, dot_nt(q2, k_ref[0, :, lanes])).astype(bf16)
        w_ref[p] = weights
        att_ref[:, lanes] = dot(beside(weights), heads(v_ref[0, :, lanes]))


def attend_kernel(len_ref, q_ref, g_ref, gain_ref, att_ref, *refs):
    c_refs, (out_ref, ga_ref), state_refs = refs[:GROUP], refs[GROUP : GROUP + 2], refs[GROUP + 2 : -1]
    part_ref = refs[-1]
    r, _ = place()
    before = before_mask(bounds(len_ref))
    same = (lax.broadcasted_iota(i32, (PAIR, PAIR), 0) < E) == left_lanes(PAIR)
    ones = jnp.where(same, 1.0 / E, 0.0).astype(bf16)
    ones2 = jnp.concatenate([ones, ones], axis=0)
    todo = list(local_pairs(r))
    for first in range(0, PAIRS, BATCHED):
        some = todo[first : first + BATCHED]
        qbs = [pick(before, q_ref[0, :, lanes]) for _, _, _, lanes in some]
        atts = [
            att_ref[:, lanes] + dot(qb, heads(c_refs[o][rows, :]))
            for qb, (o, rows, _, lanes) in zip(qbs, some)
        ]
        dys = [g_ref[0, :, lanes].astype(f32) for _, _, _, lanes in some]
        ds = [dy * gain_ref[:, lanes] for dy, (_, _, _, lanes) in zip(dys, some)]
        means = [
            dot(jnp.concatenate(split(jnp.concatenate([att * att, d * att], axis=0)), axis=1), ones2)
            for att, d in zip(atts, ds)
        ]
        gas = []
        for att, dy, d, mean, (_, _, pair, lanes) in zip(atts, dys, ds, means, some):
            root = lax.rsqrt(mean[:BLK] + eps)
            normed = att * root
            out_ref[0, :, lanes] = (gain_ref[:, lanes] * normed).astype(bf16)
            ga = ((d - normed * (mean[BLK:] * root)) * root).astype(bf16)
            ga_ref[:, lanes] = ga
            part_ref[pl.ds(pair, 1), :] = jnp.sum(dy * normed, axis=0, keepdims=True)
            gas.append(ga)
        fulls = [dot_tn(qb, ga) for qb, ga in zip(qbs, gas)]
        for full, (o, rows, _, _) in zip(fulls, some):
            state_refs[o][rows, :] = fold(full).astype(bf16)
    tile = jnp.concatenate(split(part_ref[...]), axis=0)
    for ref in state_refs[1:]:
        ref[ROWS:] = tile


def grads_kernel(len_ref, q_ref, k_ref, v_ref, w_ref, ga_ref, *refs):
    c_refs, (gq_ref, pk_ref, pv_ref) = refs[:GROUP], refs[GROUP:]
    r, _ = place()
    begins = bounds(len_ref)
    mask, before = pair_mask(begins), before_mask(begins)
    todo = list(local_pairs(r))
    for first in range(0, PAIRS, BATCHED):
        some = todo[first : first + BATCHED]
        ga2s = [heads(ga_ref[:, lanes]) for _, _, _, lanes in some]
        gws = [
            pick(mask, dot_nt(ga2, v_ref[0, :, pair[3]])).astype(bf16) for ga2, pair in zip(ga2s, some)
        ]
        gqs = [
            dot(beside(gw), heads(k_ref[0, :, lanes]))
            + dot_nt(pick(before, ga_ref[:, lanes]), heads(c_refs[o][rows, :]))
            for gw, (o, rows, _, lanes) in zip(gws, some)
        ]
        for gq, gw, ga2, (_, _, pair, lanes) in zip(gqs, gws, ga2s, some):
            gq_ref[0, :, lanes] = gq.astype(bf16)
            pk_ref[:, lanes] = dot_tn(gw, heads(q_ref[0, :, lanes]))
            pv_ref[:, lanes] = dot_tn(w_ref[pair], ga2)


def last_kernel(len_ref, k_ref, v_ref, pk_ref, pv_ref, *refs):
    c_refs, (gk_ref, gv_ref) = refs[:GROUP], refs[GROUP:]
    r, _ = place()
    after = after_mask(bounds(len_ref))
    for o, rows, _, lanes in local_pairs(r):
        k = pick(after, k_ref[0, :, lanes])
        v = pick(after, v_ref[0, :, lanes])
        carried = heads(c_refs[o][rows, :])
        gk_ref[0, :, lanes] = (pk_ref[:, lanes] + dot_nt(v, carried)).astype(bf16)
        gv_ref[0, :, lanes] = (pv_ref[:, lanes] + dot(k, carried)).astype(bf16)


def call(kernel, outs, n_in, name, scratch=()):
    vmem = pl.BlockSpec(memory_space=pltpu.VMEM)
    smem = pl.BlockSpec(memory_space=pltpu.SMEM)
    return pl.pallas_call(
        kernel,
        out_shape=outs,
        in_specs=[smem] + [vmem] * n_in,
        out_specs=jax.tree.map(lambda _: vmem, outs),
        scratch_shapes=list(scratch),
        compiler_params=pltpu.CompilerParams(vmem_limit_bytes=48 << 20),
        name=name,
    )


def exchange(arrays):
    count = lax.axis_size("ctx")
    got = [
        lax.ppermute(arrays[o], "ctx", [(i, i ^ o) for i in range(count)])
        for o in range(GROUP - 1, 0, -1)
    ]
    return [arrays[0]] + got[::-1]


def chain(lengths, states, back, part=None, beside=()):
    shape = jax.ShapeDtypeStruct
    share, wide = shape((ROWS, PAIR), bf16), shape((ROWS + TILE, PAIR), bf16)
    terms, four = shape((PAIRS, PAIR), f32), shape((GROUP * PAIRS, PAIR), f32)
    name = "back" if back else "ahead"
    stage = pltpu.VMEM((GROUP, ROWS, PAIR), bf16)
    count = lax.axis_size("ctx")
    states = exchange(states)
    extra = (part,) if back else ()
    total = call(
        total_kernel(back), wide if back else share, GROUP + len(extra), name + "_total", [stage]
    )(lengths, *states, *extra)
    step = -GROUP if back else GROUP
    far = [
        lax.ppermute(total, "ctx", [(i, (i + d * step) % count) for i in range(count)])
        for d in range(REACH, 0, -1)
    ][::-1]
    if not back:
        outs = call(carry_kernel(False), (share,) * GROUP, GROUP + REACH, name + "_carry", [stage] * 2)(
            lengths, *states, *far
        )
        return exchange(outs), None, beside
    far, beside = lax.optimization_barrier((far, beside))
    *outs, mine = call(
        carry_kernel(True), (share,) * GROUP + (four,), GROUP + REACH + 1, name + "_carry", [stage] * 2
    )(lengths, *states, *far, total)
    theirs = lax.ppermute(mine, "ctx", [(i, (i + count // 2) % count) for i in range(count)])
    gains = call(
        gather_kernel, terms, 2, "gather", [pltpu.VMEM((count // GROUP, PAIRS, PAIR), f32)]
    )(lengths, mine, theirs)
    outs = exchange(outs)
    gains, *outs = lax.optimization_barrier((gains, *outs))
    return outs, gains, beside


def over_dp(gains):
    count = lax.axis_size("dp")
    step = 1
    while step < count:
        gains = gains + lax.ppermute(gains, "dp", [(i, i ^ step) for i in range(count)])
        step *= 2
    return gains


def per_device(queries, keys, values, grad_output, out_gain, doc_lengths):
    shape = jax.ShapeDtypeStruct
    full = shape(queries.shape, bf16)
    plain = shape((BLK, H * E), f32)
    share = shape((ROWS, PAIR), bf16)
    wide = shape((ROWS + TILE, PAIR), bf16)
    gain = out_gain.reshape(1, H * E)
    states = call(own_state_kernel, (share,) * GROUP, 2, "own_state")(doc_lengths, keys, values)
    weights, inside = call(
        inside_kernel, (shape((PAIRS, 2 * BLK, BLK), bf16), plain), 3, "inside"
    )(doc_lengths, queries, keys, values)
    carried, _, _ = chain(doc_lengths, states, False)
    output, grad_att, *states, part = call(
        attend_kernel,
        (full, shape((BLK, H * E), bf16), share, wide, wide, wide, shape((PAIRS, PAIR), f32)),
        4 + GROUP,
        "attend",
    )(doc_lengths, queries, grad_output, gain, inside, *carried)
    parts = call(grads_kernel, (full, plain, plain), 5 + GROUP, "grads")(
        doc_lengths, queries, keys, values, weights, grad_att, *carried
    )
    carried, gains, parts = chain(doc_lengths, states, True, part, parts)
    grad_q, part_k, part_v = parts
    grad_k, grad_v = call(last_kernel, (full, full), 4 + GROUP, "last")(
        doc_lengths, keys, values, part_k, part_v, *carried
    )
    total_tokens = lax.axis_size("dp") * BLK * lax.axis_size("ctx")
    grad_gain = over_dp(gains).reshape(H * E) / math.sqrt(total_tokens)
    return (output, grad_q, grad_k, grad_v, grad_gain)


def solution(mesh):
    spread = P("dp", "ctx", None)
    return jax.shard_map(
        per_device,
        mesh=mesh,
        in_specs=(spread, spread, spread, spread, P(), P("dp", None)),
        out_specs=(spread, spread, spread, spread, P()),
        check_vma=False,
    )
```
